32 devices in a mesh: seq: 8 (over z, core), chan: 4 (over y, x).
Axes of the slice: x: 2, y: 2, z: 4, core: 2. Of those that a mesh axis runs over, the one named last changes fastest.
Arguments:
- hidden: bfloat16 [4096, 2560], P('seq'), may hold values from -16 to 16
- embedding: bfloat16 [4096, 2560], P('seq'), may hold values from -16 to 16
- segments: int32 [4096], replicated, may hold values from 0 to 2, never falling along the last dimension, each value on 1 to 3072 neighbouring positions
- input_norm_gain: float32 [2560], replicated, may hold values from 0.5 to 1.5
- gate_proj: bfloat16 [2560, 5120], P(None, 'chan'), may hold values from -0.125 to 0.125
- input_proj: bfloat16 [2560, 5120], P(None, 'chan'), may hold values from -0.125 to 0.125
- state_proj: bfloat16 [2560, 128], replicated, may hold values from -0.125 to 0.125
- step_proj: bfloat16 [2560, 80], P(None, 'chan'), may hold values from -1 to 1
- step_bias: float32 [80], P('chan'), may hold values from -5 to -3
- decay_log: float32 [80], P('chan'), may hold values from -8 to 1
- skip_gain: float32 [80], P('chan'), may hold values from 0.5 to 1.5
- out_gain: float32 [5120], P('chan'), may hold values from 0.5 to 1.5
- out_proj: bfloat16 [5120, 2560], P('chan'), may hold values from -0.078125 to 0.078125
- attn_gain: float32 [5120], replicated, may hold values from 0.5 to 1.5
- query_proj: bfloat16 [5120, 5120], P('seq', 'chan'), may hold values from -1 to 1
- key_proj: bfloat16 [5120, 5120], P('seq', 'chan'), may hold values from -1 to 1
- value_proj: bfloat16 [5120, 5120], P('seq', 'chan'), may hold values from -0.078125 to 0.078125
- attn_out: bfloat16 [5120, 2560], P('chan', 'seq'), may hold values from -0.078125 to 0.078125
Outputs:
- mixed: bfloat16 [4096, 2560], P('seq', 'chan')
The draws below stay inside these ranges and needn't reach their ends.
Inputs may be any that keep to these rules, and one draw needn't show every extreme that they name: `segments`: document ids never fall along the sequence, and every document has 1 to 3072 positions.
All inputs are finite; a program needn't handle non-finite values.
Results may differ from the reference program's by a relative error of at most 0.0095.
Values may be sent and summed in bfloat16 or wider, within the bound.
A program may use at most 256 MiB of HBM per device.

```python
import math
import jax
import jax.numpy as jnp
import numpy as np
from jax import lax

D = 2560
N = 64
HEAD_CHANNELS = 64
AH = 32
DI = 5120
H = 80
AP = 160
TOK_DEV = 512
SEQUENCE_TOKENS = 4096


def spike_weights(key):
    source = jax.random.normal(jax.random.fold_in(key, 7), (D, H), jnp.float32)
    return jnp.clip(source, -6.0, 6.0) / math.sqrt(D)


def drawn_weight(key, salt):
    source = jnp.clip(jax.random.normal(jax.random.fold_in(key, salt), (2 * D, 2 * D), jnp.float32), -6.0, 6.0)
    values = source / math.sqrt(2 * D)
    return values


def draw_query_proj(key, part):
    return drawn_weight(key, 32).astype(jnp.bfloat16)


def draw_key_proj(key, part):
    return drawn_weight(key, 33).astype(jnp.bfloat16)


def draw_embedding(key, part):
    values = jnp.clip(jax.random.normal(jax.random.fold_in(key, 31), (SEQUENCE_TOKENS, D), jnp.float32), -6.0, 6.0)
    return jnp.clip(values, -16.0, 16.0).astype(jnp.bfloat16)


def draw_step_proj(key, part):
    return spike_weights(key).astype(jnp.bfloat16)


def draw_hidden(key, part):
    source = jnp.clip(jax.random.normal(jax.random.fold_in(key, 3), (SEQUENCE_TOKENS, D), jnp.float32), -6.0, 6.0)
    heading_vector = jnp.sum(spike_weights(key), axis=1)
    heading_vector = heading_vector / jnp.sqrt(jnp.mean(heading_vector * heading_vector))
    spots = jax.random.randint(jax.random.fold_in(key, 5), (6,), 0, SEQUENCE_TOKENS)
    marks = jnp.zeros((SEQUENCE_TOKENS,), jnp.float32).at[spots].set(1.0)
    values = source * (1.0 - 0.7 * marks[:, None]) + 3.0 * marks[:, None] * heading_vector[None, :]
    return jnp.clip(values, -16.0, 16.0).astype(jnp.bfloat16)


def draw_decay_log(key, part):
    order = jax.random.permutation(jax.random.fold_in(key, 1), H)
    slow_count = H // 2
    slower = (order < slow_count).astype(jnp.float32)
    unit = jax.random.uniform(jax.random.fold_in(key, 2), (H,), jnp.float32)
    slow_rate = jnp.log(0.2 / (0.02 * SEQUENCE_TOKENS)) + unit * jnp.log(5.0)
    fast_rate = -0.7 + unit * 1.7
    values = slower * slow_rate + (1.0 - slower) * fast_rate
    return values


def block_levels(key, dims, cuts, least, largest):
    level = 1.0
    for dim, parts in cuts:
        draws = jax.random.uniform(jax.random.fold_in(jax.random.fold_in(key, 6), dim), (parts,), jnp.float32, least / len(cuts), largest / len(cuts))
        level = level * jnp.repeat(jnp.exp(draws), dims[dim] // parts).reshape((-1,) + (1,) * (len(dims) - 1 - dim))
    return level


def profile(amount, total, most, lean):
    portions = [(1 << 20) // math.isqrt(rank ** lean) + 1 for rank in range(2, amount + 1)]
    surplus, counts = total - most - (amount - 1), [1] * (amount - 1)
    while surplus > 0:
        candidates = [i for i in range(amount - 1) if counts[i] < most]
        whole, left = sum([portions[i] for i in candidates]), surplus
        for i in candidates:
            addition = min(most - counts[i], max(1, left * portions[i] // whole), surplus)
            counts[i] = counts[i] + addition
            surplus = surplus - addition
    return np.array([most] + counts)


def ragged_sizes(stream_key, number_of, total, most, slope):
    if number_of == 2:
        one = jax.random.randint(stream_key, (), max(1, total - most), min(most, total - 1) + 1)
        return jnp.stack([one, total - one])
    lengths = jnp.asarray(profile(number_of, total, most, slope), jnp.int32)
    pairs = (number_of - 1) // 2
    giver, sink = lengths[1:1 + 2 * pairs:2], lengths[2:2 + 2 * pairs:2]
    margin = jnp.minimum(giver - 1, most - sink)
    moved = jax.random.randint(jax.random.fold_in(stream_key, 1), (pairs,), 0, 1 << 20) % (margin + 1)
    lengths = lengths.at[1:1 + 2 * pairs:2].set(giver - moved).at[2:2 + 2 * pairs:2].set(sink + moved)
    return lengths[jax.random.permutation(jax.random.fold_in(stream_key, 2), number_of)]


def scatter_about(stream_key, shape, width, most, split=(), kind=jnp.bfloat16):
    entries = width * jax.random.normal(stream_key, shape, jnp.float32)
    if split:
        entries = entries * block_levels(stream_key, shape, split, -0.22, 0.18)
    return jnp.clip(entries, -most, most).astype(kind)


def setup_inputs(seed: int = 0) -> dict:
    keys = jax.random.split(jax.random.key(seed), 19)
    hidden = draw_hidden(jax.random.fold_in(keys[18], 71), 0)
    embedding = draw_embedding(jax.random.fold_in(keys[18], 71), 0)
    segments = jnp.searchsorted(jnp.cumsum(ragged_sizes(keys[2], 3, SEQUENCE_TOKENS, 3 * SEQUENCE_TOKENS // 4, 0)), jnp.arange(SEQUENCE_TOKENS), side="right").astype(jnp.int32)
    input_norm_gain = jnp.clip(1.0 + 0.1 * jax.random.normal(keys[3], (D,), jnp.float32), 0.5, 1.5)
    gate_proj = scatter_about(keys[4], (D, DI), D ** -0.5, 0.125, ((1, 4),))
    input_proj = scatter_about(keys[5], (D, DI), D ** -0.5, 0.125, ((1, 4),))
    state_proj = scatter_about(keys[6], (D, 2 * N), D ** -0.5, 0.125)
    step_proj = draw_step_proj(jax.random.fold_in(keys[18], 71), 0)
    step_bias = jnp.clip(-5.0 + 2.0 * jax.random.uniform(keys[8], (H,), jnp.float32) ** block_levels(keys[8], (H,), ((0, 4),), -0.2, 0.2), -5.0, -3.0)
    decay_log = draw_decay_log(jax.random.fold_in(keys[18], 71), 0)
    skip_gain = jnp.clip(0.5 + 1.0 * jax.random.uniform(keys[10], (H,), jnp.float32) ** block_levels(keys[10], (H,), ((0, 4),), -0.2, 0.2), 0.5, 1.5)
    out_gain = jnp.clip(1.0 + 0.1 * jax.random.normal(keys[11], (DI,), jnp.float32), 0.5, 1.5)
    out_proj = scatter_about(keys[12], (DI, D), DI ** -0.5, 0.078125, ((0, 4),))
    attn_gain = jnp.clip(1.0 + 0.1 * jax.random.normal(keys[13], (2 * D,), jnp.float32), 0.5, 1.5)
    query_proj = draw_query_proj(jax.random.fold_in(keys[18], 71), 0)
    key_proj = draw_key_proj(jax.random.fold_in(keys[18], 71), 0)
    value_proj = scatter_about(keys[16], (2 * D, 2 * D), (2 * D) ** -0.5, 0.078125, ((0, 8), (1, 4)))
    attn_out = scatter_about(keys[17], (2 * D, D), (2 * D) ** -0.5, 0.078125, ((0, 4), (1, 8)))
    return dict(hidden=hidden, embedding=embedding, segments=segments, input_norm_gain=input_norm_gain, gate_proj=gate_proj, input_proj=input_proj, state_proj=state_proj, step_proj=step_proj, step_bias=step_bias, decay_log=decay_log, skip_gain=skip_gain, out_gain=out_gain, out_proj=out_proj, attn_gain=attn_gain, query_proj=query_proj, key_proj=key_proj, value_proj=value_proj, attn_out=attn_out)


EPSILON = 1e-05
HIGHEST = lax.Precision.HIGHEST

def normalize(values_in, gain_in):
    widened = values_in.astype(jnp.float32)
    factor = lax.rsqrt(lax.optimization_barrier(jnp.mean(widened * widened, axis=-1, keepdims=True)) + EPSILON)
    return (widened * factor * gain_in).astype(jnp.bfloat16)

def block_terms(inputs_x, steps_dt, rate_vec, b_rows, c_rows, doc_ids, prev_doc):
    block_len = inputs_x.shape[0]
    head_count = steps_dt.shape[1]
    per_head = inputs_x.shape[1] // head_count
    logdecay = steps_dt * rate_vec[None, :]
    running = jnp.cumsum(logdecay, axis=0)
    places = jnp.arange(block_len)
    allowed = (places[:, None] >= places[None, :]) & (doc_ids[:, None] == doc_ids[None, :])
    spread = running.T[:, :, None] - running.T[:, None, :]
    decays = jnp.exp(jnp.where(allowed[None], spread, -1e+30))
    intersection = jnp.dot(c_rows, b_rows.T, precision=HIGHEST)
    scaled_x = inputs_x.reshape(block_len, head_count, per_head) * steps_dt[:, :, None]
    intra_out = jnp.einsum('hts,shp->thp', decays * intersection[None], scaled_x, precision=HIGHEST)
    final_doc = doc_ids[block_len - 1]
    keeping = jnp.exp(running[block_len - 1][None, :] - running) * (doc_ids == final_doc).astype(jnp.float32)[:, None]
    own_state = jnp.einsum('sn,shp->hnp', b_rows, scaled_x * keeping[:, :, None], precision=HIGHEST)
    through = jnp.exp(running[block_len - 1]) * (final_doc == prev_doc).astype(jnp.float32)
    entering = jnp.exp(running) * (doc_ids == prev_doc).astype(jnp.float32)[:, None]
    return (intra_out, own_state, through, entering)

def carried(c_rows, entering, state_in):
    return jnp.einsum('tn,hnp->thp', c_rows, state_in, precision=HIGHEST) * entering[:, :, None]

def reference(hidden, embedding, segments, input_norm_gain, gate_proj, input_proj, state_proj, step_proj, step_bias, decay_log, skip_gain, out_gain, out_proj, attn_gain, query_proj, key_proj, value_proj, attn_out):
    tokens_n = normalize(hidden, input_norm_gain)
    gate_z = jnp.dot(tokens_n, gate_proj, preferred_element_type=jnp.float32)
    inputs_x = jax.nn.silu(jnp.dot(tokens_n, input_proj, preferred_element_type=jnp.float32))
    b_and_c = jax.nn.silu(jnp.dot(tokens_n, state_proj, preferred_element_type=jnp.float32))
    b_rows = b_and_c[:, :N]
    c_rows = b_and_c[:, N:]
    steps_dt = jax.nn.softplus(jnp.dot(tokens_n, step_proj, preferred_element_type=jnp.float32) + step_bias[None, :])
    rate_vec = -jnp.exp(decay_log)
    blocks = SEQUENCE_TOKENS // TOK_DEV

    def advance(carry, pieces):
        state, prev_doc = carry
        piece_x, piece_dt, piece_b, piece_c, document_index = pieces
        intra_out, own_state, through, entering = block_terms(piece_x, piece_dt, rate_vec, piece_b, piece_c, document_index, prev_doc)
        outputs = intra_out + carried(piece_c, entering, state)
        return ((through[:, None, None] * state + own_state, document_index[TOK_DEV - 1]), outputs)
    start_state = jnp.zeros((H, N, HEAD_CHANNELS), jnp.float32)
    final_carry, mixed_y = lax.scan(advance, (start_state, jnp.int32(-1)), (inputs_x.reshape(blocks, TOK_DEV, DI), steps_dt.reshape(blocks, TOK_DEV, H), b_rows.reshape(blocks, TOK_DEV, N), c_rows.reshape(blocks, TOK_DEV, N), segments.reshape(blocks, TOK_DEV)))
    y_full = mixed_y.reshape(SEQUENCE_TOKENS, DI) + inputs_x * jnp.repeat(skip_gain, HEAD_CHANNELS)[None, :]
    gated = y_full * jax.nn.silu(gate_z)
    squares = lax.optimization_barrier(jnp.sum(gated * gated, axis=-1, keepdims=True))
    weighted = (gated * out_gain[None, :]).astype(jnp.bfloat16)
    partial_value = jnp.dot(weighted, out_proj, preferred_element_type=jnp.float32)
    mamba_out = partial_value * lax.rsqrt(squares / DI + EPSILON)
    mixed_h = (hidden.astype(jnp.float32) + mamba_out).astype(jnp.bfloat16)
    joined = jnp.concatenate((mixed_h, embedding), axis=1)
    attention_input = normalize(joined, attn_gain)
    queries = jnp.dot(attention_input, query_proj, preferred_element_type=jnp.float32).astype(jnp.bfloat16)
    keys_all = jnp.dot(attention_input, key_proj, preferred_element_type=jnp.float32).astype(jnp.bfloat16)
    values_all = jnp.dot(attention_input, value_proj, preferred_element_type=jnp.float32).astype(jnp.bfloat16)
    places = jnp.arange(SEQUENCE_TOKENS)
    visible = (places[None, :] <= places[:, None]) & (segments[None, :] == segments[:, None])

    def one_head(trio):
        query_head, key_head, value_head = trio
        scores = jnp.dot(query_head, key_head.T, preferred_element_type=jnp.float32) * AP ** (-0.5)
        scores = jnp.where(visible, scores, -1e+30)
        row_max = lax.optimization_barrier(jnp.max(scores, axis=-1, keepdims=True))
        weights = jnp.where(visible, jnp.exp(scores - row_max), 0.0)
        row_sum = lax.optimization_barrier(jnp.sum(weights, axis=-1, keepdims=True))
        return jnp.dot(weights.astype(jnp.bfloat16), value_head, preferred_element_type=jnp.float32) / row_sum
    contexts = lax.map(one_head, (queries.reshape(SEQUENCE_TOKENS, AH, AP).transpose(1, 0, 2), keys_all.reshape(SEQUENCE_TOKENS, AH, AP).transpose(1, 0, 2), values_all.reshape(SEQUENCE_TOKENS, AH, AP).transpose(1, 0, 2)))
    context = contexts.transpose(1, 0, 2).reshape(SEQUENCE_TOKENS, 2 * D).astype(jnp.bfloat16)
    result = jnp.dot(context, attn_out, preferred_element_type=jnp.float32) + mixed_h.astype(jnp.float32)
    return result.astype(jnp.bfloat16)
```

```python
import functools

import jax
import jax.numpy as jnp
from jax import lax
from jax.experimental import pallas as pl
from jax.experimental.pallas import tpu as pltpu
from jax.sharding import PartitionSpec as P

N = 64
HEAD_CHANNELS = 64
AP = 160

EPSILON = 1e-05
HIGHEST = lax.Precision.HIGHEST
LOG2E = 1.4426950408889634


def normalize(values_in, gain_in):
    widened = values_in.astype(jnp.float32)
    factor = lax.rsqrt(jnp.mean(widened * widened, axis=-1, keepdims=True) + EPSILON)
    return (widened * factor * gain_in).astype(jnp.bfloat16)


def partner_of(index, shift, count):
    return index ^ shift if count & (count - 1) == 0 else (index + shift) % count


def exchange(value, axis, shift, count):
    return lax.ppermute(value, axis, [(i, partner_of(i, shift, count)) for i in range(count)])


def source_of(index, shift, count):
    return index ^ shift if count & (count - 1) == 0 else (index - shift) % count


def reduce_columns(rows, weight, axis, here, count):
    width = weight.shape[1] // count

    def part(owner):
        cols = lax.dynamic_slice_in_dim(weight, owner * width, width, 1)
        return jnp.dot(rows, cols, preferred_element_type=jnp.float32)

    arrived = [
        exchange(part(partner_of(here, shift, count)).astype(jnp.bfloat16), axis, shift, count)
        for shift in range(count - 1, 0, -1)
    ]
    total = part(here)
    for piece in arrived:
        total = total + piece.astype(jnp.float32)
    return total


def gather_columns(share, axis, here, count):
    width = share.shape[1]
    full = jnp.zeros((share.shape[0], width * count), share.dtype)
    full = lax.dynamic_update_slice_in_dim(full, share, here * width, 1)
    for shift in range(1, count):
        piece = exchange(share, axis, shift, count)
        full = lax.dynamic_update_slice_in_dim(full, piece, source_of(here, shift, count) * width, 1)
    return full


def pair_stack(value, core, count):
    other = lax.ppermute(value, "seq", [(i, i ^ 1) for i in range(count)])
    first = jnp.where(core == 0, value, other)
    second = jnp.where(core == 0, other, value)
    return jnp.concatenate((first, second), axis=0)


def flash_kernel(step, chunk, scale, low_ref, offset_ref, q_ref, start_ref, k_ref, v_ref, o_ref):
    block = pl.program_id(1)
    first_row = offset_ref[0] + block * step
    q = q_ref[0]
    starts = start_ref[...]

    def scores_of(c, diagonal):
        keys = k_ref[0, pl.ds(pl.multiple_of(c * chunk, chunk), chunk), :]
        s = lax.dot_general(q, keys, (((1,), (1,)), ((), ())), preferred_element_type=jnp.float32)
        places = c * chunk + lax.broadcasted_iota(jnp.int32, (step, chunk), 1)
        seen = places >= starts
        if diagonal:
            rows = first_row + lax.broadcasted_iota(jnp.int32, (step, chunk), 0)
            seen = seen & (places <= rows)
        return jnp.where(seen, s * scale, -1e30)

    def take(c, carry, diagonal=False):
        top, total, acc = carry
        s = scores_of(c, diagonal)
        new_top = jnp.maximum(top, jnp.max(s, axis=1, keepdims=True))
        shrink = jnp.exp2(top - new_top)
        w = jnp.exp2(s - new_top)
        total = total * shrink + jnp.sum(w, axis=1, keepdims=True)
        vals = v_ref[0, pl.ds(pl.multiple_of(c * chunk, chunk), chunk), :]
        acc = acc * shrink + jnp.dot(w.astype(jnp.bfloat16), vals, preferred_element_type=jnp.float32)
        return new_top, total, acc

    carry = (
        jnp.full((step, 1), -1e30, jnp.float32),
        jnp.zeros((step, 1), jnp.float32),
        jnp.zeros((step, q.shape[1]), jnp.float32),
    )
    own = first_row // chunk
    carry = take(own, carry, True)
    top, total, acc = lax.fori_loop(low_ref[block], own, take, carry)
    o_ref[0] = (acc / total).astype(o_ref.dtype)


def attend(queries, keys, values, starts, offset):
    heads, rows, width = queries.shape
    depth = keys.shape[1]
    step = 512 if rows % 512 == 0 else rows
    lows = starts[::step] // step
    grid_spec = pltpu.PrefetchScalarGridSpec(
        num_scalar_prefetch=2,
        grid=(heads, rows // step),
        in_specs=[
            pl.BlockSpec((1, step, width), lambda h, b, *_: (h, b, 0)),
            pl.BlockSpec((step, 1), lambda h, b, *_: (b, 0)),
            pl.BlockSpec((1, depth, width), lambda h, b, *_: (h, 0, 0)),
            pl.BlockSpec((1, depth, width), lambda h, b, *_: (h, 0, 0)),
        ],
        out_specs=pl.BlockSpec((1, step, width), lambda h, b, *_: (h, b, 0)),
    )
    return pl.pallas_call(
        functools.partial(flash_kernel, step, step, width ** (-0.5) * LOG2E),
        out_shape=jax.ShapeDtypeStruct(queries.shape, jnp.bfloat16),
        grid_spec=grid_spec,
        compiler_params=pltpu.CompilerParams(vmem_limit_bytes=48 * 1024 * 1024),
        cost_estimate=pl.CostEstimate(
            flops=2 * heads * rows * depth * width, bytes_accessed=8 * heads * depth * width, transcendentals=0
        ),
        name="attend",
    )(lows.astype(jnp.int32), offset.reshape(1).astype(jnp.int32), queries, starts[:, None], keys, values)


def block_terms(inputs_x, steps_dt, rate_vec, b_rows, c_rows, doc_ids, prev_doc):
    block_len = inputs_x.shape[0]
    head_count = steps_dt.shape[1]
    per_head = inputs_x.shape[1] // head_count
    logdecay = steps_dt * rate_vec[None, :]
    running = jnp.cumsum(logdecay, axis=0)
    places = jnp.arange(block_len)
    allowed = (places[:, None] >= places[None, :]) & (doc_ids[:, None] == doc_ids[None, :])
    spread = running.T[:, :, None] - running.T[:, None, :]
    decays = jnp.exp(jnp.where(allowed[None], spread, -1e30))
    intersection = jnp.dot(c_rows, b_rows.T, precision=HIGHEST)
    scaled_x = inputs_x.reshape(block_len, head_count, per_head) * steps_dt[:, :, None]
    intra_out = jnp.einsum("hts,shp->thp", decays * intersection[None], scaled_x, precision=HIGHEST)
    final_doc = doc_ids[block_len - 1]
    keeping = (
        jnp.exp(running[block_len - 1][None, :] - running)
        * (doc_ids == final_doc).astype(jnp.float32)[:, None]
    )
    own_state = jnp.einsum("sn,shp->hnp", b_rows, scaled_x * keeping[:, :, None], precision=HIGHEST)
    through = jnp.exp(running[block_len - 1]) * (final_doc == prev_doc).astype(jnp.float32)
    entering = jnp.exp(running) * (doc_ids == prev_doc).astype(jnp.float32)[:, None]
    return (intra_out, own_state, through, entering)


def carried(c_rows, entering, state_in):
    return jnp.einsum("tn,hnp->thp", c_rows, state_in, precision=HIGHEST) * entering[:, :, None]


def earlier_states(through, own_state, count):
    heads = through.shape[0]
    flat = own_state.reshape(heads, -1).astype(jnp.bfloat16)
    total = jnp.zeros(own_state.shape, jnp.float32)
    between = jnp.ones_like(through)
    for shift in range(1, count):
        routes = [(i, i + shift) for i in range(count - shift)]
        state = lax.ppermute(flat, "seq", routes).astype(jnp.float32).reshape(own_state.shape)
        total = total + between[:, None, None] * state
        if shift < count - 1:
            between = between * lax.ppermute(through, "seq", routes)
    return total


def local(
    hidden,
    embedding,
    segments,
    input_norm_gain,
    gate_proj,
    input_proj,
    state_proj,
    step_proj,
    step_bias,
    decay_log,
    skip_gain,
    out_gain,
    out_proj,
    attn_gain,
    query_proj,
    key_proj,
    value_proj,
    attn_out,
):
    tok_rows = hidden.shape[0]
    seq_index = lax.axis_index("seq")
    chan_index = lax.axis_index("chan")
    seq_count = lax.axis_size("seq")
    chan_count = lax.axis_size("chan")
    row_start = seq_index * tok_rows
    core = seq_index % 2
    chips = seq_count // 2
    chip = seq_index // 2
    pairs = [[2 * i, 2 * i + 1] for i in range(chips)]
    lines = [[2 * i + c for i in range(chips)] for c in range(2)]
    head_cols = query_proj.shape[1]
    core_cols = head_cols // 2
    core_heads = core_cols // AP

    def own_half(weight):
        kept = lax.dynamic_slice_in_dim(weight, core * core_cols, core_cols, 1)
        given = lax.dynamic_slice_in_dim(weight, (1 - core) * core_cols, core_cols, 1)
        other = lax.ppermute(given, "seq", [(i, i ^ 1) for i in range(seq_count)])
        first = jnp.where(core == 0, kept, other)
        second = jnp.where(core == 0, other, kept)
        block = jnp.concatenate((first, second), axis=0)
        return lax.all_gather(block, "seq", axis=0, tiled=True, axis_index_groups=lines)

    value_all, key_all, query_all = (own_half(w) for w in (value_proj, key_proj, query_proj))
    out_cols = lax.all_gather(attn_out, "seq", axis=1, tiled=True)
    embedding_both = pair_stack(embedding, core, seq_count)

    tokens_n = normalize(hidden, input_norm_gain)
    inputs_x = jax.nn.silu(jnp.dot(tokens_n, input_proj, preferred_element_type=jnp.float32))
    b_and_c = jax.nn.silu(jnp.dot(tokens_n, state_proj, preferred_element_type=jnp.float32))
    b_rows = b_and_c[:, :N]
    c_rows = b_and_c[:, N:]
    steps_dt = jax.nn.softplus(
        jnp.dot(tokens_n, step_proj, preferred_element_type=jnp.float32) + step_bias[None, :]
    )
    rate_vec = -jnp.exp(decay_log)
    doc_ids = lax.dynamic_slice_in_dim(segments, row_start, tok_rows)
    before = lax.dynamic_slice_in_dim(segments, jnp.maximum(row_start - 1, 0), 1)[0]
    prev_doc = jnp.where(seq_index > 0, before, -1)
    intra_out, own_state, through, entering = block_terms(
        inputs_x, steps_dt, rate_vec, b_rows, c_rows, doc_ids, prev_doc
    )
    state_in = earlier_states(through, own_state, seq_count)
    gate_z = jnp.dot(tokens_n, gate_proj, preferred_element_type=jnp.float32)
    mixed_y = intra_out + carried(c_rows, entering, state_in)
    y_full = (
        mixed_y.reshape(tok_rows, -1) + inputs_x * jnp.repeat(skip_gain, HEAD_CHANNELS)[None, :]
    )
    gated = y_full * jax.nn.silu(gate_z)
    squares = jnp.sum(gated * gated, axis=-1)
    weighted = (gated * out_gain[None, :]).astype(jnp.bfloat16)
    inner_total = gate_proj.shape[1] * chan_count
    feat_width = hidden.shape[1] // chan_count
    square_total = squares
    for shift in range(1, chan_count):
        square_total = square_total + exchange(squares, "chan", shift, chan_count)
    shares = reduce_columns(weighted, out_proj, "chan", chan_index, chan_count)
    own_cols = lax.dynamic_slice_in_dim(hidden, chan_index * feat_width, feat_width, 1)
    mixed_share = (
        own_cols.astype(jnp.float32)
        + shares * lax.rsqrt(square_total / inner_total + EPSILON)[:, None]
    ).astype(jnp.bfloat16)
    mixed_h = gather_columns(mixed_share, "chan", chan_index, chan_count)
    mixed_both = pair_stack(mixed_h, core, seq_count)
    joined = jnp.concatenate((mixed_both, embedding_both), axis=1)
    attention_input = normalize(joined, attn_gain)

    chip_rows = 2 * tok_rows
    places = jnp.arange(segments.shape[0], dtype=jnp.int32)
    starts = jnp.min(
        jnp.where(segments[None, :] == segments[:, None], places[None, :], segments.shape[0]), axis=1
    )

    def heads_of(weight):
        made = jnp.dot(attention_input, weight, preferred_element_type=jnp.float32).astype(jnp.bfloat16)
        return made.reshape(chip_rows, core_heads, AP).transpose(1, 0, 2)

    by_head = core_heads % chips == 0
    if by_head:

        def spread_heads(weight):
            return lax.all_to_all(
                heads_of(weight), "seq", split_axis=0, concat_axis=1, tiled=True, axis_index_groups=lines
            )

        values, keys, queries = (spread_heads(w) for w in (value_all, key_all, query_all))
        context = attend(queries, keys, values, starts, jnp.zeros((), jnp.int32))
        context = lax.all_to_all(context, "seq", split_axis=1, concat_axis=0, tiled=True)
        mine = core_heads // chips
        context = context.reshape(chips, 2, mine, tok_rows, AP).transpose(3, 1, 0, 2, 4)
    else:
        values, keys, queries = (heads_of(w) for w in (value_all, key_all, query_all))
        keys, values = (
            lax.all_gather(part, "seq", axis=1, tiled=True, axis_index_groups=lines) for part in (keys, values)
        )
        offset = chip * chip_rows
        own_starts = lax.dynamic_slice_in_dim(starts, offset, chip_rows)
        context = attend(queries, keys, values, own_starts, offset)
        context = lax.all_to_all(
            context, "seq", split_axis=1, concat_axis=0, tiled=True, axis_index_groups=pairs
        )
        context = context.transpose(1, 0, 2)
    context = context.reshape(tok_rows, head_cols)
    out_share = reduce_columns(context, out_cols, "chan", chan_index, chan_count)
    own_mixed = lax.dynamic_slice_in_dim(mixed_h, chan_index * feat_width, feat_width, 1)
    return (out_share + own_mixed.astype(jnp.float32)).astype(jnp.bfloat16)


def solution(mesh):
    in_specs = (
        P("seq", None),
        P("seq", None),
        P(),
        P(),
        P(None, "chan"),
        P(None, "chan"),
        P(),
        P(None, "chan"),
        P("chan"),
        P("chan"),
        P("chan"),
        P("chan"),
        P("chan", None),
        P(),
        P("seq", "chan"),
        P("seq", "chan"),
        P("seq", "chan"),
        P("chan", "seq"),
    )
    out_specs = P("seq", "chan")
    return jax.shard_map(local, mesh=mesh, in_specs=in_specs, out_specs=out_specs, check_vma=False)
```
